32 devices in a mesh: row: 4 (over y, x), col: 8 (over z, core).
Axes of the slice: x: 2, y: 2, z: 4, core: 2. Of those that a mesh axis runs over, the one named last changes fastest.
Arguments:
- history: bfloat16 [2, 4096, 4096], P(None, 'row', 'col'), may hold values from -2 to 2, as said below
- start_strip: float32 [2, 2048, 4096], P(None, 'col', 'row'), may hold values from -6 to 6
- coupling: float32 [32], replicated, may hold values from 0.5 to 1.5
- dyson_inverse: float32 [2, 2, 64, 64], replicated, may hold values from -3 to 3, as said below
Outputs:
- earlier: float32 [2, 2048, 4096], P(None, None, 'col')
- later: float32 [2, 2048, 4096], P(None, 'col', 'row')
The draws below stay inside these ranges and needn't reach their ends.
Inputs may be any that keep to these rules, and one draw needn't show every extreme that they name: history is anti-Hermitian: its element at row (s, a), column (t, b) is minus the complex conjugate of its element at row (t, b), column (s, a). `dyson_inverse`: each group's inverse is lower triangular in time.
All inputs are finite; a program needn't handle non-finite values.
Results may differ from the reference program's by a relative error of at most 0.0043.
Values may be sent and summed in bfloat16 or wider, within the bound.
A program may use at most 192 MiB of HBM per device.

```python
import math
import jax
import jax.numpy as jnp
from jax import lax

NO = 32
C = 64
NT = 128


def draw_history(key, part):
    width = NT * NO
    key_real = jax.random.fold_in(key, 11)
    key_imag = jax.random.fold_in(key, 12)
    noise_real = jax.random.normal(key_real, (width, width), jnp.float32) * width ** (-0.5)
    noise_imag = jax.random.normal(key_imag, (width, width), jnp.float32) * width ** (-0.5)
    real_part = (noise_real - noise_real.T) * 0.5
    imag_part = (noise_imag + noise_imag.T) * 0.5
    return jnp.stack([real_part, imag_part]).astype(jnp.bfloat16)


def draw_dyson_inverse(key, part):
    key_real = jax.random.fold_in(key, 21)
    key_imag = jax.random.fold_in(key, 22)
    lower = jnp.tril(jnp.ones((C, C), jnp.float32))
    noise_real = jax.random.normal(key_real, (2, C, C), jnp.float32) * (0.5 * C ** (-0.5))
    noise_imag = jax.random.normal(key_imag, (2, C, C), jnp.float32) * (0.5 * C ** (-0.5))
    real_part = jnp.eye(C, dtype=jnp.float32)[None] + noise_real * lower[None]
    imag_part = noise_imag * lower[None]
    return jnp.stack([real_part, imag_part], axis=1)


def levels(own_key, dims, shards, least, high):
    level = 1.0
    for axis_at, blocks in shards:
        steps = jax.random.uniform(jax.random.fold_in(jax.random.fold_in(own_key, 6), axis_at), (blocks,), jnp.float32, least / len(shards), high / len(shards))
        level = level * jnp.repeat(jnp.exp(steps), dims[axis_at] // blocks).reshape((-1,) + (1,) * (len(dims) - 1 - axis_at))
    return level


def normal_values(own_key, dims, scale, limit, shards=(), kind=jnp.bfloat16):
    loudness = levels(own_key, dims, shards, -0.22, 0.18) if shards else 1.0
    array = jax.random.normal(own_key, dims, jnp.float32) * scale * loudness
    return jnp.minimum(jnp.maximum(array, -limit), limit).astype(kind)


def setup_inputs(seed: int = 0) -> dict:
    splits = jax.random.split(jax.random.key(seed), 5)
    history = draw_history(jax.random.fold_in(splits[4], 71), 0)
    start_strip = normal_values(splits[1], (2, C * NO, NT * NO), 1.0, 6.0, ((1, 8), (2, 4)), jnp.float32)
    coupling = jnp.clip(jnp.exp(jax.random.uniform(splits[2], (NO,), jnp.float32, math.log(0.5), math.log(1.5))), 0.5, 1.5)
    dyson_inverse = draw_dyson_inverse(jax.random.fold_in(splits[4], 71), 0)
    return {"history": history, "start_strip": start_strip, "coupling": coupling, "dyson_inverse": dyson_inverse}


TIME_STEP = 0.15


def complex_product(first_pair, second_pair):
    real_out = jnp.dot(first_pair[0], second_pair[0], precision=lax.Precision.HIGHEST, preferred_element_type=jnp.float32) - jnp.dot(first_pair[1], second_pair[1], precision=lax.Precision.HIGHEST, preferred_element_type=jnp.float32)
    imag_out = jnp.dot(first_pair[0], second_pair[1], precision=lax.Precision.HIGHEST, preferred_element_type=jnp.float32) + jnp.dot(first_pair[1], second_pair[0], precision=lax.Precision.HIGHEST, preferred_element_type=jnp.float32)
    return jnp.stack([real_out, imag_out])


def self_energy(green, row_weight, col_weight):
    magnitude = green[0] * green[0] + green[1] * green[1]
    factor = -(row_weight[:, None] * col_weight[None, :]) * magnitude
    return green * factor[None]


def dyson_apply(inverse, source):
    group_len = inverse.shape[1]
    flat_width = source.shape[1] * source.shape[2] // group_len
    flat = source.reshape(2, group_len, flat_width)
    real_out = jnp.dot(inverse[0], flat[0], precision=lax.Precision.HIGHEST, preferred_element_type=jnp.float32) - jnp.dot(inverse[1], flat[1], precision=lax.Precision.HIGHEST, preferred_element_type=jnp.float32)
    imag_out = jnp.dot(inverse[0], flat[1], precision=lax.Precision.HIGHEST, preferred_element_type=jnp.float32) + jnp.dot(inverse[1], flat[0], precision=lax.Precision.HIGHEST, preferred_element_type=jnp.float32)
    return jnp.stack([real_out, imag_out]).reshape(source.shape)


def reference(history, start_strip, coupling, dyson_inverse):
    hist_wide = history.astype(jnp.float32)
    row_weight = jnp.tile(coupling, C)
    col_weight = jnp.tile(coupling, NT)
    sigma_first = self_energy(start_strip, row_weight, col_weight).astype(jnp.bfloat16)
    sigma_first = lax.optimization_barrier(sigma_first).astype(jnp.float32)
    earlier = dyson_apply(dyson_inverse[0], TIME_STEP * complex_product(sigma_first, hist_wide))
    sigma_second = self_energy(earlier, row_weight, col_weight).astype(jnp.bfloat16)
    sigma_second = lax.optimization_barrier(sigma_second).astype(jnp.float32)
    later = dyson_apply(dyson_inverse[1], TIME_STEP * complex_product(sigma_second, hist_wide))
    return earlier, later
```

```python
import functools

import jax
import jax.numpy as jnp
from jax import lax
from jax.experimental import pallas as pl
from jax.experimental.pallas import tpu as pltpu
from jax.sharding import PartitionSpec as P

TIME_STEP = 0.15


def complex_product(first_pair, second_pair):
    real_out = jnp.dot(first_pair[0], second_pair[0], preferred_element_type=jnp.float32) - jnp.dot(
        first_pair[1], second_pair[1], preferred_element_type=jnp.float32
    )
    imag_out = jnp.dot(first_pair[0], second_pair[1], preferred_element_type=jnp.float32) + jnp.dot(
        first_pair[1], second_pair[0], preferred_element_type=jnp.float32
    )
    return jnp.stack([real_out, imag_out])


def mirror_product(sigma_pair, tile_pair):
    contract = (((1,), (1,)), ((), ()))
    real_real = lax.dot_general(
        sigma_pair[0], tile_pair[0], contract, preferred_element_type=jnp.float32
    )
    imag_imag = lax.dot_general(
        sigma_pair[1], tile_pair[1], contract, preferred_element_type=jnp.float32
    )
    real_imag = lax.dot_general(
        sigma_pair[0], tile_pair[1], contract, preferred_element_type=jnp.float32
    )
    imag_real = lax.dot_general(
        sigma_pair[1], tile_pair[0], contract, preferred_element_type=jnp.float32
    )
    return jnp.stack([-real_real - imag_imag, real_imag - imag_real])


def self_energy(green, row_weight, col_weight):
    magnitude = green[0] * green[0] + green[1] * green[1]
    factor = -(row_weight[:, None] * col_weight[None, :]) * magnitude
    return green * factor[None]


def orbital_weights(coupling, offset, count):
    orbitals = coupling.shape[0]
    position = (offset + jnp.arange(count, dtype=jnp.int32)) % orbitals
    one_hot = (position[:, None] == jnp.arange(orbitals, dtype=jnp.int32)[None, :]).astype(
        jnp.float32
    )
    return jnp.dot(
        one_hot, coupling, precision=lax.Precision.HIGHEST, preferred_element_type=jnp.float32
    )


def dyson_apply(inverse, source):
    group_len = inverse.shape[1]
    flat_width = source.shape[1] * source.shape[2] // group_len
    flat = source.reshape(2, group_len, flat_width)
    real_out = jnp.dot(
        inverse[0], flat[0], precision=lax.Precision.HIGHEST, preferred_element_type=jnp.float32
    ) - jnp.dot(
        inverse[1], flat[1], precision=lax.Precision.HIGHEST, preferred_element_type=jnp.float32
    )
    imag_out = jnp.dot(
        inverse[0], flat[1], precision=lax.Precision.HIGHEST, preferred_element_type=jnp.float32
    ) + jnp.dot(
        inverse[1], flat[0], precision=lax.Precision.HIGHEST, preferred_element_type=jnp.float32
    )
    return jnp.stack([real_out, imag_out]).reshape(source.shape)


MESH = pl.DeviceIdType.MESH
NN = (((1,), (0,)), ((), ()))
NT = (((1,), (1,)), ((), ()))


def mm(x, y, dims):
    return lax.dot_general(x, y, dims, preferred_element_type=jnp.float32)


def remote(src, dst, send_sem, recv_sem, row, col):
    return pltpu.make_async_remote_copy(
        src_ref=src,
        dst_ref=dst,
        send_sem=send_sem,
        recv_sem=recv_sem,
        device_id=(row, col),
        device_id_type=MESH,
    )


def entry_barrier(row, q, core, lines, rows):
    barrier = pltpu.get_barrier_semaphore()

    def greet(to_row, to_col):
        pl.semaphore_signal(barrier, inc=1, device_id=(to_row, to_col), device_id_type=MESH)

    greet(row, 2 * q + 1 - core)
    for k in range(1, rows):
        greet(lax.rem(row + k, rows), 2 * q + core)

    @pl.when(q > 0)
    def _():
        greet(row, 2 * (q - 1) + core)

    @pl.when(q < lines - 1)
    def _():
        greet(row, 2 * (q + 1) + core)

    ends = jnp.minimum(q, 1) + jnp.minimum(lines - 1 - q, 1)
    pl.semaphore_wait(barrier, rows + ends)


def first_kernel(lines, rows, sig, hist, out, blocks, parts, recv, local, hop_s, hop_r, pair_s, pair_r, sum_s, sum_r):
    row = lax.axis_index("row")
    col = lax.axis_index("col")
    q, core = lax.div(col, 2), lax.rem(col, 2)
    strip = sig.shape[1]
    share = out.shape[2]
    entry_barrier(row, q, core, lines, rows)

    own = pltpu.make_async_copy(sig, blocks.at[col], local)
    own.start()
    own.wait()

    def hop(way, s):
        step = 1 - 2 * way
        block = blocks.at[2 * (q - step * s) + core]
        return remote(block, block, hop_s.at[way, s], hop_r.at[way, s], row, 2 * (q + step) + core)

    def sends(way, s):
        if way == 0:
            return jnp.logical_and(q < lines - 1, q - s >= 0)
        return jnp.logical_and(q > 0, q + s <= lines - 1)

    def arrived(way, s):
        if way == 0:
            return q - 1 - s >= 0
        return q + 1 + s <= lines - 1

    def origin(way, s):
        step = 1 - 2 * way
        return q - step * (s + 1)

    def pair(line, at):
        block = blocks.at[2 * line + core]
        return remote(block, block, pair_s.at[at], pair_r.at[at], row, 2 * q + 1 - core)

    def spread(j, k):
        to = lax.rem(row + k, rows)
        return remote(
            parts.at[j, to], recv.at[j, k - 1], sum_s.at[j, k - 1], sum_r.at[j, k - 1], to, col
        )

    def compute(j):
        real = mm(blocks[j, 0], hist[0], NN) - mm(blocks[j, 1], hist[1], NN)
        imag = mm(blocks[j, 0], hist[1], NN) + mm(blocks[j, 1], hist[0], NN)
        at = pl.ds(pl.multiple_of(j * strip, strip), strip)
        for r in range(rows):
            cut = slice(r * share, (r + 1) * share)
            parts[j, r, 0] = real[:, cut].astype(jnp.bfloat16)
            parts[j, r, 1] = imag[:, cut].astype(jnp.bfloat16)

            @pl.when(row == r)
            def _():
                out[0, at, :] = real[:, cut]
                out[1, at, :] = imag[:, cut]

        for k in range(1, rows):
            spread(j, k).start()

    for way in (0, 1):

        @pl.when(sends(way, 0))
        def _():
            hop(way, 0).start()

    pair(q, 2 * (lines - 1)).start()

    def own_step(i, c):
        @pl.when(i == 1)
        def _():
            pair(q, 2 * (lines - 1)).wait_recv()

        compute(2 * q + core + i - 2 * core * i)
        return c

    lax.fori_loop(0, 2, own_step, 0)

    def step(s, c):
        for way in (0, 1):

            @pl.when(arrived(way, s))
            def _():
                hop(way, s).wait_recv()
                pair(origin(way, s), 2 * s + way).start()

            @pl.when(jnp.logical_and(s < lines - 2, sends(way, s + 1)))
            def _():
                hop(way, s + 1).start()

        def each(i, c2):
            way, other = lax.rem(i, 2), lax.div(i, 2)
            line = q - (1 - 2 * way) * (s + 1)

            @pl.when(jnp.logical_and(line >= 0, line <= lines - 1))
            def _():
                @pl.when(other == 1)
                def _():
                    pair(line, 2 * s + way).wait_recv()

                compute(2 * line + core + other - 2 * core * other)

            return c2

        lax.fori_loop(0, 4, each, 0)
        return c

    lax.fori_loop(0, lines - 1, step, 0)

    def finish(j, c):
        at = pl.ds(pl.multiple_of(j * strip, strip), strip)
        for k in range(1, rows):
            spread(j, k).wait_recv()
        for p in (0, 1):
            total = out[p, at, :]
            for k in range(1, rows):
                total += recv[j, k - 1, p].astype(jnp.float32)
            out[p, at, :] = total
        for k in range(1, rows):
            spread(j, k).wait_send()
        return c

    lax.fori_loop(0, 2 * lines, finish, 0)
    pair(q, 2 * (lines - 1)).wait_send()

    def drain(s, c):
        for way in (0, 1):

            @pl.when(sends(way, s))
            def _():
                hop(way, s).wait_send()

            @pl.when(arrived(way, s))
            def _():
                pair(origin(way, s), 2 * s + way).wait_send()

        return c

    lax.fori_loop(0, lines - 1, drain, 0)


def second_kernel(lines, tau, hist, out, give, take, stage, land, pair_s, pair_r, hop_s, hop_r):
    row = lax.axis_index("row")
    col = lax.axis_index("col")
    q, core = lax.div(col, 2), lax.rem(col, 2)
    strip = out.shape[1]
    entry_barrier(row, q, core, lines, 1)

    def product(j):
        at = pl.ds(pl.multiple_of(j * strip, strip), strip)
        real_in, imag_in = tau[0, at, :], tau[1, at, :]
        real = -mm(real_in, hist[0], NT) - mm(imag_in, hist[1], NT)
        imag = mm(real_in, hist[1], NT) - mm(imag_in, hist[0], NT)
        return real, imag

    def pair(d):
        return remote(
            give.at[d], take.at[d], pair_s.at[d], pair_r.at[d], row, 2 * q + 1 - core
        )

    def hop(way, d):
        to = q + 1 - 2 * way
        return remote(
            stage.at[d], land.at[way, d], hop_s.at[d], hop_r.at[way, d], row, 2 * to + core
        )

    def offer(d):
        real, imag = product(2 * d + 1 - core)
        give[d, 0] = real.astype(jnp.bfloat16)
        give[d, 1] = imag.astype(jnp.bfloat16)
        pair(d).start()

    def gather(d):
        real, imag = product(2 * d + core)
        out[0] = real
        out[1] = imag
        pair(d).wait_recv()
        for p in (0, 1):
            out[p] += take[d, p].astype(jnp.float32)

    def add(way, d):
        hop(way, d).wait_recv()
        for p in (0, 1):
            out[p] += land[way, d, p].astype(jnp.float32)

    def step(i, c):
        t, way = lax.div(i, 2), lax.rem(i, 2)
        d = (lines - 1 - t) * (1 - way) + t * way
        far = (d - q) * (1 - 2 * way)

        @pl.when(far > 0)
        def _():
            offer(d)
            gather(d)

            @pl.when(jnp.logical_and(way == 0, q > 0))
            def _():
                add(0, d)

            @pl.when(jnp.logical_and(way == 1, q < lines - 1))
            def _():
                add(1, d)

            for p in (0, 1):
                stage[d, p] = out[p].astype(jnp.bfloat16)
            hop(way, d).start()

        return c

    lax.fori_loop(0, 2 * (lines - 1), step, 0)
    offer(q)
    gather(q)

    @pl.when(q > 0)
    def _():
        add(0, q)

    @pl.when(q < lines - 1)
    def _():
        add(1, q)

    def drain(d, c):
        pair(d).wait_send()

        @pl.when(d > q)
        def _():
            hop(0, d).wait_send()

        @pl.when(d < q)
        def _():
            hop(1, d).wait_send()

        return c

    lax.fori_loop(0, lines, drain, 0)


VMEM = pl.BlockSpec(memory_space=pltpu.VMEM)
DMA = pltpu.SemaphoreType.DMA


def first_sums(sigma, history, lines, rows):
    strip, depth = sigma.shape[1:]
    cols = 2 * lines
    share = history.shape[2] // rows
    bf16 = jnp.bfloat16
    return pl.pallas_call(
        functools.partial(first_kernel, lines, rows),
        out_shape=jax.ShapeDtypeStruct((2, strip * cols, share), jnp.float32),
        in_specs=[VMEM] * 2,
        out_specs=VMEM,
        scratch_shapes=[
            pltpu.VMEM((cols, 2, strip, depth), bf16),
            pltpu.VMEM((cols, rows, 2, strip, share), bf16),
            pltpu.VMEM((cols, rows - 1, 2, strip, share), bf16),
            DMA,
            DMA((2, lines - 1)),
            DMA((2, lines - 1)),
            DMA((2 * lines - 1,)),
            DMA((2 * lines - 1,)),
            DMA((cols, rows - 1)),
            DMA((cols, rows - 1)),
        ],
        compiler_params=pltpu.CompilerParams(
            collective_id=0, has_side_effects=True, vmem_limit_bytes=40 * 1024 * 1024
        ),
        name="first_sums",
    )(sigma, history)


def second_sums(tau, history, lines):
    depth = history.shape[1]
    strip = tau.shape[1] // (2 * lines)
    bf16 = jnp.bfloat16
    return pl.pallas_call(
        functools.partial(second_kernel, lines),
        out_shape=jax.ShapeDtypeStruct((2, strip, depth), jnp.float32),
        in_specs=[VMEM] * 2,
        out_specs=VMEM,
        scratch_shapes=[
            pltpu.VMEM((lines, 2, strip, depth), bf16),
            pltpu.VMEM((lines, 2, strip, depth), bf16),
            pltpu.VMEM((lines, 2, strip, depth), bf16),
            pltpu.VMEM((2, lines, 2, strip, depth), bf16),
            DMA((lines,)),
            DMA((lines,)),
            DMA((lines,)),
            DMA((2, lines)),
        ],
        compiler_params=pltpu.CompilerParams(
            collective_id=1, has_side_effects=True, vmem_limit_bytes=50 * 1024 * 1024
        ),
        name="second_sums",
    )(tau, history)


def shards(history, start_strip, coupling, dyson_inverse):
    row_count = lax.axis_size("row")
    col_count = lax.axis_size("col")
    row_index = lax.axis_index("row")
    col_index = lax.axis_index("col")
    strip_rows = start_strip.shape[1]
    strip_cols = start_strip.shape[2]
    group_rows = strip_rows * col_count
    tile_cols = history.shape[2]
    sigma_first = self_energy(
        start_strip,
        orbital_weights(coupling, col_index * strip_rows, strip_rows),
        orbital_weights(coupling, row_index * strip_cols, strip_cols),
    ).astype(jnp.bfloat16)
    if tile_cols // row_count % 128 == 0:
        shares = first_sums(sigma_first, history, col_count // 2, row_count)
    else:
        partial_first = complex_product(
            lax.all_gather(sigma_first, "col", axis=1, tiled=True), history
        )
        shares = lax.psum_scatter(partial_first, "row", scatter_dimension=2, tiled=True)
    solved_part = dyson_apply(dyson_inverse[0], TIME_STEP * shares)
    earlier = lax.all_gather(solved_part, "row", axis=2, tiled=True)
    sigma_second = self_energy(
        earlier,
        orbital_weights(coupling, 0, group_rows),
        orbital_weights(coupling, col_index * tile_cols, tile_cols),
    ).astype(jnp.bfloat16)
    solved_sigma = dyson_apply(
        dyson_inverse[1], TIME_STEP * sigma_second.astype(jnp.float32)
    ).astype(jnp.bfloat16)
    later_strip = second_sums(solved_sigma, history, col_count // 2)
    return (earlier, later_strip)


def solution(mesh):
    return jax.shard_map(
        shards,
        mesh=mesh,
        in_specs=(P(None, "row", "col"), P(None, "col", "row"), P(), P()),
        out_specs=(P(None, None, "col"), P(None, "col", "row")),
        check_vma=False,
    )
```

```python
import functools

import jax
import jax.numpy as jnp
from jax import lax
from jax.experimental import pallas as pl
from jax.experimental.pallas import tpu as pltpu
from jax.sharding import PartitionSpec as P

TIME_STEP = 0.15


def complex_product(first_pair, second_pair):
    real_out = jnp.dot(first_pair[0], second_pair[0], preferred_element_type=jnp.float32) - jnp.dot(
        first_pair[1], second_pair[1], preferred_element_type=jnp.float32
    )
    imag_out = jnp.dot(first_pair[0], second_pair[1], preferred_element_type=jnp.float32) + jnp.dot(
        first_pair[1], second_pair[0], preferred_element_type=jnp.float32
    )
    return jnp.stack([real_out, imag_out])


def mirror_product(sigma_pair, tile_pair):
    contract = (((1,), (1,)), ((), ()))
    real_real = lax.dot_general(
        sigma_pair[0], tile_pair[0], contract, preferred_element_type=jnp.float32
    )
    imag_imag = lax.dot_general(
        sigma_pair[1], tile_pair[1], contract, preferred_element_type=jnp.float32
    )
    real_imag = lax.dot_general(
        sigma_pair[0], tile_pair[1], contract, preferred_element_type=jnp.float32
    )
    imag_real = lax.dot_general(
        sigma_pair[1], tile_pair[0], contract, preferred_element_type=jnp.float32
    )
    return jnp.stack([-real_real - imag_imag, real_imag - imag_real])


def self_energy(green, row_weight, col_weight):
    magnitude = green[0] * green[0] + green[1] * green[1]
    factor = -(row_weight[:, None] * col_weight[None, :]) * magnitude
    return green * factor[None]


def orbital_weights(coupling, offset, count):
    orbitals = coupling.shape[0]
    position = (offset + jnp.arange(count, dtype=jnp.int32)) % orbitals
    one_hot = (position[:, None] == jnp.arange(orbitals, dtype=jnp.int32)[None, :]).astype(
        jnp.float32
    )
    return jnp.dot(
        one_hot, coupling, precision=lax.Precision.HIGHEST, preferred_element_type=jnp.float32
    )


MESH = pl.DeviceIdType.MESH
NN = (((1,), (0,)), ((), ()))
NT = (((1,), (1,)), ((), ()))


def mm(x, y, dims):
    return lax.dot_general(x, y, dims, preferred_element_type=jnp.float32)


def remote(src, dst, send_sem, recv_sem, row, col):
    return pltpu.make_async_remote_copy(
        src_ref=src,
        dst_ref=dst,
        send_sem=send_sem,
        recv_sem=recv_sem,
        device_id=(row, col),
        device_id_type=MESH,
    )


def entry_barrier(row, q, core, lines, rows):
    barrier = pltpu.get_barrier_semaphore()

    def greet(to_row, to_col):
        pl.semaphore_signal(barrier, inc=1, device_id=(to_row, to_col), device_id_type=MESH)

    greet(row, 2 * q + 1 - core)
    for k in range(1, rows):
        greet(lax.rem(row + k, rows), 2 * q + core)

    @pl.when(q > 0)
    def _():
        greet(row, 2 * (q - 1) + core)

    @pl.when(q < lines - 1)
    def _():
        greet(row, 2 * (q + 1) + core)

    ends = jnp.minimum(q, 1) + jnp.minimum(lines - 1 - q, 1)
    pl.semaphore_wait(barrier, rows + ends)


def first_kernel(lines, rows, sig, hist, out, blocks, parts, recv, local, hop_s, hop_r, pair_s, pair_r, sum_s, sum_r):
    row = lax.axis_index("row")
    col = lax.axis_index("col")
    q, core = lax.div(col, 2), lax.rem(col, 2)
    strip = sig.shape[1]
    share = out.shape[2]
    entry_barrier(row, q, core, lines, rows)

    own = pltpu.make_async_copy(sig, blocks.at[col], local)
    own.start()
    own.wait()

    def hop(way, s):
        step = 1 - 2 * way
        block = blocks.at[2 * (q - step * s) + core]
        return remote(block, block, hop_s.at[way, s], hop_r.at[way, s], row, 2 * (q + step) + core)

    def sends(way, s):
        if way == 0:
            return jnp.logical_and(q < lines - 1, q - s >= 0)
        return jnp.logical_and(q > 0, q + s <= lines - 1)

    def arrived(way, s):
        if way == 0:
            return q - 1 - s >= 0
        return q + 1 + s <= lines - 1

    def origin(way, s):
        step = 1 - 2 * way
        return q - step * (s + 1)

    def pair(line, at):
        block = blocks.at[2 * line + core]
        return remote(block, block, pair_s.at[at], pair_r.at[at], row, 2 * q + 1 - core)

    def spread(j, k):
        to = lax.rem(row + k, rows)
        return remote(
            parts.at[j, to], recv.at[j, k - 1], sum_s.at[j, k - 1], sum_r.at[j, k - 1], to, col
        )

    def compute(j):
        real = mm(blocks[j, 0], hist[0], NN) - mm(blocks[j, 1], hist[1], NN)
        imag = mm(blocks[j, 0], hist[1], NN) + mm(blocks[j, 1], hist[0], NN)
        at = pl.ds(pl.multiple_of(j * strip, strip), strip)
        for r in range(rows):
            cut = slice(r * share, (r + 1) * share)
            parts[j, r, 0] = real[:, cut].astype(jnp.bfloat16)
            parts[j, r, 1] = imag[:, cut].astype(jnp.bfloat16)

            @pl.when(row == r)
            def _():
                out[0, at, :] = real[:, cut]
                out[1, at, :] = imag[:, cut]

        for k in range(1, rows):
            spread(j, k).start()

    for way in (0, 1):

        @pl.when(sends(way, 0))
        def _():
            hop(way, 0).start()

    pair(q, 2 * (lines - 1)).start()

    def own_step(i, c):
        @pl.when(i == 1)
        def _():
            pair(q, 2 * (lines - 1)).wait_recv()

        compute(2 * q + core + i - 2 * core * i)
        return c

    lax.fori_loop(0, 2, own_step, 0)

    def step(s, c):
        for way in (0, 1):

            @pl.when(arrived(way, s))
            def _():
                hop(way, s).wait_recv()
                pair(origin(way, s), 2 * s + way).start()

            @pl.when(jnp.logical_and(s < lines - 2, sends(way, s + 1)))
            def _():
                hop(way, s + 1).start()

        def each(i, c2):
            way, other = lax.rem(i, 2), lax.div(i, 2)
            line = q - (1 - 2 * way) * (s + 1)

            @pl.when(jnp.logical_and(line >= 0, line <= lines - 1))
            def _():
                @pl.when(other == 1)
                def _():
                    pair(line, 2 * s + way).wait_recv()

                compute(2 * line + core + other - 2 * core * other)

            return c2

        lax.fori_loop(0, 4, each, 0)
        return c

    lax.fori_loop(0, lines - 1, step, 0)

    def finish(j, c):
        at = pl.ds(pl.multiple_of(j * strip, strip), strip)
        for k in range(1, rows):
            spread(j, k).wait_recv()
        for p in (0, 1):
            total = out[p, at, :]
            for k in range(1, rows):
                total += recv[j, k - 1, p].astype(jnp.float32)
            out[p, at, :] = total
        for k in range(1, rows):
            spread(j, k).wait_send()
        return c

    lax.fori_loop(0, 2 * lines, finish, 0)
    pair(q, 2 * (lines - 1)).wait_send()

    def drain(s, c):
        for way in (0, 1):

            @pl.when(sends(way, s))
            def _():
                hop(way, s).wait_send()

            @pl.when(arrived(way, s))
            def _():
                pair(origin(way, s), 2 * s + way).wait_send()

        return c

    lax.fori_loop(0, lines - 1, drain, 0)


def second_kernel(
    lines, rows, tau, near, hist, out, wide, taus, give, take, stage, land,
    local, pair_s, pair_r, hop_s, hop_r, tau_s, tau_r, wide_s, wide_r,
):
    row = lax.axis_index("row")
    col = lax.axis_index("col")
    q, core = lax.div(col, 2), lax.rem(col, 2)
    half = lax.div(2 * q, lines)
    strip = out.shape[1]
    entry_barrier(row, q, core, lines, rows)

    def span(j):
        return pl.ds(pl.multiple_of(j * strip, strip), strip)

    def spread(j, k):
        return remote(
            tau.at[:, span(j)],
            taus.at[row, :, span(j)],
            tau_s.at[j, k - 1],
            tau_r.at[j, k - 1],
            lax.rem(row + k, rows),
            col,
        )

    def widen(k):
        return remote(
            near, wide.at[row], wide_s.at[k - 1], wide_r.at[k - 1], lax.rem(row + k, rows), col
        )

    def order(i):
        t, way = lax.div(i, 2), lax.rem(i + half, 2)
        d = (lines - 1 - t) * (1 - way) + t * way
        return d, way, (d - q) * (1 - 2 * way)

    def issue(d):
        for j in (2 * d + 1 - core, 2 * d + core):
            for k in range(1, rows):
                spread(j, k).start()

    def early(i, c):
        d, way, far = order(i)

        @pl.when(far > 0)
        def _():
            issue(d)

        return c

    lax.fori_loop(0, 2 * (lines - 1), early, 0)
    issue(q)
    for k in range(1, rows):
        widen(k).start()
    own_wide = pltpu.make_async_copy(near, wide.at[row], local.at[0])
    own_wide.start()
    own_tau = pltpu.make_async_copy(tau, taus.at[row], local.at[1])
    own_tau.start()
    own_tau.wait()

    def product(j):
        for k in range(1, rows):
            spread(j, k).wait_recv()
        at = span(j)
        real_in = jnp.concatenate([taus[r, 0, at, :] for r in range(rows)], axis=1)
        imag_in = jnp.concatenate([taus[r, 1, at, :] for r in range(rows)], axis=1)
        real = -mm(real_in, hist[0], NT) - mm(imag_in, hist[1], NT)
        imag = mm(real_in, hist[1], NT) - mm(imag_in, hist[0], NT)
        return real, imag

    def pair(d):
        return remote(
            give.at[d], take.at[d], pair_s.at[d], pair_r.at[d], row, 2 * q + 1 - core
        )

    def hop(way, d):
        to = q + 1 - 2 * way
        return remote(
            stage.at[d], land.at[way, d], hop_s.at[d], hop_r.at[way, d], row, 2 * to + core
        )

    def offer(d):
        real, imag = product(2 * d + 1 - core)
        give[d, 0] = real.astype(jnp.bfloat16)
        give[d, 1] = imag.astype(jnp.bfloat16)
        pair(d).start()

    def gather(d):
        real, imag = product(2 * d + core)
        out[0] = real
        out[1] = imag
        pair(d).wait_recv()
        for p in (0, 1):
            out[p] += take[d, p].astype(jnp.float32)

    def add(way, d):
        hop(way, d).wait_recv()
        for p in (0, 1):
            out[p] += land[way, d, p].astype(jnp.float32)

    def step(i, c):
        d, way, far = order(i)

        @pl.when(far > 0)
        def _():
            offer(d)
            gather(d)

            @pl.when(jnp.logical_and(way == 0, q > 0))
            def _():
                add(0, d)

            @pl.when(jnp.logical_and(way == 1, q < lines - 1))
            def _():
                add(1, d)

            for p in (0, 1):
                stage[d, p] = out[p].astype(jnp.bfloat16)
            hop(way, d).start()

        return c

    lax.fori_loop(0, 2 * (lines - 1), step, 0)
    offer(q)
    gather(q)

    @pl.when(q > 0)
    def _():
        add(0, q)

    @pl.when(q < lines - 1)
    def _():
        add(1, q)

    def drain(d, c):
        pair(d).wait_send()

        @pl.when(d > q)
        def _():
            hop(0, d).wait_send()

        @pl.when(d < q)
        def _():
            hop(1, d).wait_send()

        return c

    lax.fori_loop(0, lines, drain, 0)

    def drain_tau(j, c):
        for k in range(1, rows):
            spread(j, k).wait_send()
        return c

    lax.fori_loop(0, 2 * lines, drain_tau, 0)
    for k in range(1, rows):
        widen(k).wait()
    own_wide.wait()


VMEM = pl.BlockSpec(memory_space=pltpu.VMEM)
DMA = pltpu.SemaphoreType.DMA


def first_sums(sigma, history, lines, rows):
    strip, depth = sigma.shape[1:]
    cols = 2 * lines
    share = history.shape[2] // rows
    bf16 = jnp.bfloat16
    return pl.pallas_call(
        functools.partial(first_kernel, lines, rows),
        out_shape=jax.ShapeDtypeStruct((2, strip * cols, share), jnp.float32),
        in_specs=[VMEM] * 2,
        out_specs=VMEM,
        scratch_shapes=[
            pltpu.VMEM((cols, 2, strip, depth), bf16),
            pltpu.VMEM((cols, rows, 2, strip, share), bf16),
            pltpu.VMEM((cols, rows - 1, 2, strip, share), bf16),
            DMA,
            DMA((2, lines - 1)),
            DMA((2, lines - 1)),
            DMA((2 * lines - 1,)),
            DMA((2 * lines - 1,)),
            DMA((cols, rows - 1)),
            DMA((cols, rows - 1)),
        ],
        compiler_params=pltpu.CompilerParams(
            collective_id=0, has_side_effects=True, vmem_limit_bytes=40 * 1024 * 1024
        ),
        name="first_sums",
    )(sigma, history)


def second_sums(tau, near, history, lines, rows):
    depth = history.shape[1]
    strip = tau.shape[1] // (2 * lines)
    bf16 = jnp.bfloat16
    return pl.pallas_call(
        functools.partial(second_kernel, lines, rows),
        out_shape=(
            jax.ShapeDtypeStruct((2, strip, depth), jnp.float32),
            jax.ShapeDtypeStruct((rows,) + near.shape, bf16),
        ),
        in_specs=[VMEM] * 3,
        out_specs=(VMEM, pl.BlockSpec(memory_space=pl.ANY)),
        scratch_shapes=[
            pltpu.VMEM((rows,) + tau.shape, bf16),
            pltpu.VMEM((lines, 2, strip, depth), bf16),
            pltpu.VMEM((lines, 2, strip, depth), bf16),
            pltpu.VMEM((lines, 2, strip, depth), bf16),
            pltpu.VMEM((2, lines, 2, strip, depth), bf16),
            DMA((2,)),
            DMA((lines,)),
            DMA((lines,)),
            DMA((lines,)),
            DMA((2, lines)),
            DMA((2 * lines, rows - 1)),
            DMA((2 * lines, rows - 1)),
            DMA((rows - 1,)),
            DMA((rows - 1,)),
        ],
        compiler_params=pltpu.CompilerParams(
            collective_id=1, has_side_effects=True, vmem_limit_bytes=52 * 1024 * 1024
        ),
        name="second_sums",
    )(tau, near, history)


def stacked_dyson(inverse, source):
    group_len = inverse.shape[1]
    matrix = jnp.concatenate(
        [
            jnp.concatenate([inverse[0], -inverse[1]], axis=1),
            jnp.concatenate([inverse[1], inverse[0]], axis=1),
        ],
        axis=0,
    )
    flat = source.reshape(2 * group_len, -1)
    solved = jnp.dot(
        matrix, flat, precision=lax.Precision.HIGHEST, preferred_element_type=jnp.float32
    )
    return solved.reshape(source.shape)


def shards(history, start_strip, coupling, dyson_inverse):
    row_count = lax.axis_size("row")
    col_count = lax.axis_size("col")
    row_index = lax.axis_index("row")
    col_index = lax.axis_index("col")
    strip_rows = start_strip.shape[1]
    strip_cols = start_strip.shape[2]
    group_rows = strip_rows * col_count
    tile_cols = history.shape[2]
    share_cols = tile_cols // row_count
    sigma_first = self_energy(
        start_strip,
        orbital_weights(coupling, col_index * strip_rows, strip_rows),
        orbital_weights(coupling, row_index * strip_cols, strip_cols),
    ).astype(jnp.bfloat16)
    fits = share_cols % 128 == 0
    if fits:
        shares = first_sums(sigma_first, history, col_count // 2, row_count)
    else:
        partial_first = complex_product(
            lax.all_gather(sigma_first, "col", axis=1, tiled=True), history
        )
        shares = lax.psum_scatter(partial_first, "row", scatter_dimension=2, tiled=True)
    solved_part = stacked_dyson(dyson_inverse[0], TIME_STEP * shares)
    sigma_second = self_energy(
        solved_part,
        orbital_weights(coupling, 0, group_rows),
        orbital_weights(coupling, col_index * tile_cols + row_index * share_cols, share_cols),
    ).astype(jnp.bfloat16)
    solved_sigma = stacked_dyson(
        dyson_inverse[1], TIME_STEP * sigma_second.astype(jnp.float32)
    ).astype(jnp.bfloat16)
    if fits:
        later_strip, wide = second_sums(
            solved_sigma, solved_part.astype(jnp.bfloat16), history, col_count // 2, row_count
        )
        earlier = jnp.transpose(wide, (1, 2, 0, 3)).reshape(2, group_rows, tile_cols)
        return (earlier.astype(jnp.float32), later_strip)
    earlier = lax.all_gather(solved_part, "row", axis=2, tiled=True)
    tau = lax.all_gather(solved_sigma, "row", axis=2, tiled=True)
    partial_second = mirror_product(tau, history)
    later_strip = lax.psum_scatter(partial_second, "col", scatter_dimension=1, tiled=True)
    return (earlier, later_strip)


def solution(mesh):
    return jax.shard_map(
        shards,
        mesh=mesh,
        in_specs=(P(None, "row", "col"), P(None, "col", "row"), P(), P()),
        out_specs=(P(None, None, "col"), P(None, "col", "row")),
        check_vma=False,
    )
```

```python
import functools

import jax
import jax.numpy as jnp
from jax import lax
from jax.experimental import pallas as pl
from jax.experimental.pallas import tpu as pltpu
from jax.sharding import PartitionSpec as P

TIME_STEP = 0.15


def complex_product(first_pair, second_pair):
    real_out = jnp.dot(first_pair[0], second_pair[0], preferred_element_type=jnp.float32) - jnp.dot(
        first_pair[1], second_pair[1], preferred_element_type=jnp.float32
    )
    imag_out = jnp.dot(first_pair[0], second_pair[1], preferred_element_type=jnp.float32) + jnp.dot(
        first_pair[1], second_pair[0], preferred_element_type=jnp.float32
    )
    return jnp.stack([real_out, imag_out])


def mirror_product(sigma_pair, tile_pair):
    contract = (((1,), (1,)), ((), ()))
    real_real = lax.dot_general(
        sigma_pair[0], tile_pair[0], contract, preferred_element_type=jnp.float32
    )
    imag_imag = lax.dot_general(
        sigma_pair[1], tile_pair[1], contract, preferred_element_type=jnp.float32
    )
    real_imag = lax.dot_general(
        sigma_pair[0], tile_pair[1], contract, preferred_element_type=jnp.float32
    )
    imag_real = lax.dot_general(
        sigma_pair[1], tile_pair[0], contract, preferred_element_type=jnp.float32
    )
    return jnp.stack([-real_real - imag_imag, real_imag - imag_real])


def self_energy(green, row_weight, col_weight):
    magnitude = green[0] * green[0] + green[1] * green[1]
    factor = -(row_weight[:, None] * col_weight[None, :]) * magnitude
    return green * factor[None]


def orbital_weights(coupling, offset, count):
    orbitals = coupling.shape[0]
    position = (offset + jnp.arange(count, dtype=jnp.int32)) % orbitals
    one_hot = (position[:, None] == jnp.arange(orbitals, dtype=jnp.int32)[None, :]).astype(
        jnp.float32
    )
    return jnp.dot(
        one_hot, coupling, precision=lax.Precision.HIGHEST, preferred_element_type=jnp.float32
    )


MESH = pl.DeviceIdType.MESH
NN = (((1,), (0,)), ((), ()))
NT = (((1,), (1,)), ((), ()))


def mm(x, y, dims):
    return lax.dot_general(x, y, dims, preferred_element_type=jnp.float32)


def remote(src, dst, send_sem, recv_sem, row, col):
    return pltpu.make_async_remote_copy(
        src_ref=src,
        dst_ref=dst,
        send_sem=send_sem,
        recv_sem=recv_sem,
        device_id=(row, col),
        device_id_type=MESH,
    )


def entry_barrier(row, q, core, lines, rows):
    barrier = pltpu.get_barrier_semaphore()

    def greet(to_row, to_col):
        pl.semaphore_signal(barrier, inc=1, device_id=(to_row, to_col), device_id_type=MESH)

    greet(row, 2 * q + 1 - core)
    for k in range(1, rows):
        greet(lax.rem(row + k, rows), 2 * q + core)

    @pl.when(q > 0)
    def _():
        greet(row, 2 * (q - 1) + core)

    @pl.when(q < lines - 1)
    def _():
        greet(row, 2 * (q + 1) + core)

    ends = jnp.minimum(q, 1) + jnp.minimum(lines - 1 - q, 1)
    pl.semaphore_wait(barrier, rows + ends)


def first_kernel(lines, rows, sig, hist, out, blocks, parts, recv, local, hop_s, hop_r, pair_s, pair_r, sum_s, sum_r):
    row = lax.axis_index("row")
    col = lax.axis_index("col")
    q, core = lax.div(col, 2), lax.rem(col, 2)
    strip = sig.shape[1]
    share = out.shape[2]
    entry_barrier(row, q, core, lines, rows)

    own = pltpu.make_async_copy(sig, blocks.at[col], local)
    own.start()
    own.wait()

    def hop(way, s):
        step = 1 - 2 * way
        block = blocks.at[2 * (q - step * s) + core]
        return remote(block, block, hop_s.at[way, s], hop_r.at[way, s], row, 2 * (q + step) + core)

    def sends(way, s):
        if way == 0:
            return jnp.logical_and(q < lines - 1, q - s >= 0)
        return jnp.logical_and(q > 0, q + s <= lines - 1)

    def arrived(way, s):
        if way == 0:
            return q - 1 - s >= 0
        return q + 1 + s <= lines - 1

    def origin(way, s):
        step = 1 - 2 * way
        return q - step * (s + 1)

    def pair(line, at):
        block = blocks.at[2 * line + core]
        return remote(block, block, pair_s.at[at], pair_r.at[at], row, 2 * q + 1 - core)

    def spread(j, k):
        to = lax.rem(row + k, rows)
        return remote(
            parts.at[j, to], recv.at[j, k - 1], sum_s.at[j, k - 1], sum_r.at[j, k - 1], to, col
        )

    def compute(j):
        real = mm(blocks[j, 0], hist[0], NN) - mm(blocks[j, 1], hist[1], NN)
        imag = mm(blocks[j, 0], hist[1], NN) + mm(blocks[j, 1], hist[0], NN)
        at = pl.ds(pl.multiple_of(j * strip, strip), strip)
        for r in range(rows):
            cut = slice(r * share, (r + 1) * share)
            parts[j, r, 0] = real[:, cut].astype(jnp.bfloat16)
            parts[j, r, 1] = imag[:, cut].astype(jnp.bfloat16)

            @pl.when(row == r)
            def _():
                out[0, at, :] = real[:, cut]
                out[1, at, :] = imag[:, cut]

        for k in range(1, rows):
            spread(j, k).start()

    for way in (0, 1):

        @pl.when(sends(way, 0))
        def _():
            hop(way, 0).start()

    pair(q, 2 * (lines - 1)).start()

    def own_step(i, c):
        @pl.when(i == 1)
        def _():
            pair(q, 2 * (lines - 1)).wait_recv()

        compute(2 * q + core + i - 2 * core * i)
        return c

    lax.fori_loop(0, 2, own_step, 0)

    def step(s, c):
        for way in (0, 1):

            @pl.when(arrived(way, s))
            def _():
                hop(way, s).wait_recv()
                pair(origin(way, s), 2 * s + way).start()

            @pl.when(jnp.logical_and(s < lines - 2, sends(way, s + 1)))
            def _():
                hop(way, s + 1).start()

        def each(i, c2):
            way, other = lax.rem(i, 2), lax.div(i, 2)
            line = q - (1 - 2 * way) * (s + 1)

            @pl.when(jnp.logical_and(line >= 0, line <= lines - 1))
            def _():
                @pl.when(other == 1)
                def _():
                    pair(line, 2 * s + way).wait_recv()

                compute(2 * line + core + other - 2 * core * other)

            return c2

        lax.fori_loop(0, 4, each, 0)
        return c

    lax.fori_loop(0, lines - 1, step, 0)

    def finish(j, c):
        at = pl.ds(pl.multiple_of(j * strip, strip), strip)
        for k in range(1, rows):
            spread(j, k).wait_recv()
        for p in (0, 1):
            total = out[p, at, :]
            for k in range(1, rows):
                total += recv[j, k - 1, p].astype(jnp.float32)
            out[p, at, :] = total
        for k in range(1, rows):
            spread(j, k).wait_send()
        return c

    lax.fori_loop(0, 2 * lines, finish, 0)
    pair(q, 2 * (lines - 1)).wait_send()

    def drain(s, c):
        for way in (0, 1):

            @pl.when(sends(way, s))
            def _():
                hop(way, s).wait_send()

            @pl.when(arrived(way, s))
            def _():
                pair(origin(way, s), 2 * s + way).wait_send()

        return c

    lax.fori_loop(0, lines - 1, drain, 0)


def second_kernel(
    lines, rows, tau, near, hist, out, wide, taus, give, take, stage, land,
    local, pair_s, pair_r, hop_s, hop_r, tau_s, tau_r, wide_s, wide_r,
):
    row = lax.axis_index("row")
    col = lax.axis_index("col")
    q, core = lax.div(col, 2), lax.rem(col, 2)
    half = lax.div(2 * q, lines)
    strip = out.shape[1]
    entry_barrier(row, q, core, lines, rows)

    def span(j):
        return pl.ds(pl.multiple_of(j * strip, strip), strip)

    def spread(j, k):
        return remote(
            tau.at[:, span(j)],
            taus.at[row, :, span(j)],
            tau_s.at[j, k - 1],
            tau_r.at[j, k - 1],
            lax.rem(row + k, rows),
            col,
        )

    share = near.shape[2]
    mesh_2x2 = rows == 4
    beside = row + 1 - 2 * lax.rem(row, 2)
    across = lax.rem(row + 2, 4)
    direct = [beside, across] if mesh_2x2 else [lax.rem(row + k, rows) for k in range(1, rows)]

    def columns(r):
        return pl.ds(pl.multiple_of(r * share, share), share)

    mine = wide.at[:, :, columns(row)]

    def widen(k):
        return remote(near, mine, wide_s.at[k], wide_r.at[k], direct[k], col)

    def relay(k):
        block = wide.at[k, :, columns(direct[k])]
        return remote(block, block, wide_s.at[2 + k], wide_r.at[2 + k], direct[1 - k], col)

    def order(i):
        t, way = lax.div(i, 2), lax.rem(i + half, 2)
        d = (lines - 1 - t) * (1 - way) + t * way
        return d, way, (d - q) * (1 - 2 * way)

    def issue(d):
        for j in (2 * d + 1 - core, 2 * d + core):
            for k in range(1, rows):
                spread(j, k).start()

    def early(i, c):
        d, way, far = order(i)

        @pl.when(far > 0)
        def _():
            issue(d)

        return c

    lax.fori_loop(0, 2 * (lines - 1), early, 0)
    issue(q)
    for k in range(len(direct)):
        widen(k).start()
    own_wide = pltpu.make_async_copy(near, mine, local.at[0])
    own_wide.start()
    own_tau = pltpu.make_async_copy(tau, taus.at[row], local.at[1])
    own_tau.start()
    own_tau.wait()

    def product(j):
        for k in range(1, rows):
            spread(j, k).wait_recv()
        at = span(j)
        real_in = jnp.concatenate([taus[r, 0, at, :] for r in range(rows)], axis=1)
        imag_in = jnp.concatenate([taus[r, 1, at, :] for r in range(rows)], axis=1)
        real = -mm(real_in, hist[0], NT) - mm(imag_in, hist[1], NT)
        imag = mm(real_in, hist[1], NT) - mm(imag_in, hist[0], NT)
        return real, imag

    def pair(d):
        return remote(
            give.at[d], take.at[d], pair_s.at[d], pair_r.at[d], row, 2 * q + 1 - core
        )

    def hop(way, d):
        to = q + 1 - 2 * way
        return remote(
            stage.at[d], land.at[way, d], hop_s.at[d], hop_r.at[way, d], row, 2 * to + core
        )

    def offer(d):
        real, imag = product(2 * d + 1 - core)
        give[d, 0] = real.astype(jnp.bfloat16)
        give[d, 1] = imag.astype(jnp.bfloat16)
        pair(d).start()

    def gather(d):
        real, imag = product(2 * d + core)
        out[0] = real
        out[1] = imag
        pair(d).wait_recv()
        for p in (0, 1):
            out[p] += take[d, p].astype(jnp.float32)

    def add(way, d):
        hop(way, d).wait_recv()
        for p in (0, 1):
            out[p] += land[way, d, p].astype(jnp.float32)

    def step(i, c):
        d, way, far = order(i)

        @pl.when(far > 0)
        def _():
            offer(d)
            gather(d)

            @pl.when(jnp.logical_and(way == 0, q > 0))
            def _():
                add(0, d)

            @pl.when(jnp.logical_and(way == 1, q < lines - 1))
            def _():
                add(1, d)

            for p in (0, 1):
                stage[d, p] = out[p].astype(jnp.bfloat16)
            hop(way, d).start()

        return c

    lax.fori_loop(0, 2 * (lines - 1), step, 0)
    if mesh_2x2:
        for k in (0, 1):
            widen(k).wait_recv()
        for k in (0, 1):
            relay(k).start()
    offer(q)
    gather(q)

    @pl.when(q > 0)
    def _():
        add(0, q)

    @pl.when(q < lines - 1)
    def _():
        add(1, q)

    def drain(d, c):
        pair(d).wait_send()

        @pl.when(d > q)
        def _():
            hop(0, d).wait_send()

        @pl.when(d < q)
        def _():
            hop(1, d).wait_send()

        return c

    lax.fori_loop(0, lines, drain, 0)

    def drain_tau(j, c):
        for k in range(1, rows):
            spread(j, k).wait_send()
        return c

    lax.fori_loop(0, 2 * lines, drain_tau, 0)
    for k in range(len(direct)):
        widen(k).wait_send()
        if mesh_2x2:
            relay(k).wait()
        else:
            widen(k).wait_recv()
    own_wide.wait()


VMEM = pl.BlockSpec(memory_space=pltpu.VMEM)
DMA = pltpu.SemaphoreType.DMA


def first_sums(sigma, history, lines, rows):
    strip, depth = sigma.shape[1:]
    cols = 2 * lines
    share = history.shape[2] // rows
    bf16 = jnp.bfloat16
    return pl.pallas_call(
        functools.partial(first_kernel, lines, rows),
        out_shape=jax.ShapeDtypeStruct((2, strip * cols, share), jnp.float32),
        in_specs=[VMEM] * 2,
        out_specs=VMEM,
        scratch_shapes=[
            pltpu.VMEM((cols, 2, strip, depth), bf16),
            pltpu.VMEM((cols, rows, 2, strip, share), bf16),
            pltpu.VMEM((cols, rows - 1, 2, strip, share), bf16),
            DMA,
            DMA((2, lines - 1)),
            DMA((2, lines - 1)),
            DMA((2 * lines - 1,)),
            DMA((2 * lines - 1,)),
            DMA((cols, rows - 1)),
            DMA((cols, rows - 1)),
        ],
        compiler_params=pltpu.CompilerParams(
            collective_id=0, has_side_effects=True, vmem_limit_bytes=40 * 1024 * 1024
        ),
        name="first_sums",
    )(sigma, history)


def second_sums(tau, near, history, lines, rows):
    depth = history.shape[1]
    strip = tau.shape[1] // (2 * lines)
    bf16 = jnp.bfloat16
    return pl.pallas_call(
        functools.partial(second_kernel, lines, rows),
        out_shape=(
            jax.ShapeDtypeStruct((2, strip, depth), jnp.float32),
            jax.ShapeDtypeStruct(near.shape[:2] + (rows * near.shape[2],), bf16),
        ),
        in_specs=[VMEM] * 3,
        out_specs=(VMEM, pl.BlockSpec(memory_space=pl.ANY)),
        scratch_shapes=[
            pltpu.VMEM((rows,) + tau.shape, bf16),
            pltpu.VMEM((lines, 2, strip, depth), bf16),
            pltpu.VMEM((lines, 2, strip, depth), bf16),
            pltpu.VMEM((lines, 2, strip, depth), bf16),
            pltpu.VMEM((2, lines, 2, strip, depth), bf16),
            DMA((2,)),
            DMA((lines,)),
            DMA((lines,)),
            DMA((lines,)),
            DMA((2, lines)),
            DMA((2 * lines, rows - 1)),
            DMA((2 * lines, rows - 1)),
            DMA((max(rows - 1, 4),)),
            DMA((max(rows - 1, 4),)),
        ],
        compiler_params=pltpu.CompilerParams(
            collective_id=1, has_side_effects=True, vmem_limit_bytes=52 * 1024 * 1024
        ),
        name="second_sums",
    )(tau, near, history)


def stacked_dyson(inverse, source):
    group_len = inverse.shape[1]
    matrix = TIME_STEP * jnp.concatenate(
        [
            jnp.concatenate([inverse[0], -inverse[1]], axis=1),
            jnp.concatenate([inverse[1], inverse[0]], axis=1),
        ],
        axis=0,
    )
    flat = source.reshape(2 * group_len, -1)
    solved = jnp.dot(
        matrix, flat, precision=lax.Precision.HIGHEST, preferred_element_type=jnp.float32
    )
    return solved.reshape(source.shape)


def shards(history, start_strip, coupling, dyson_inverse):
    row_count = lax.axis_size("row")
    col_count = lax.axis_size("col")
    row_index = lax.axis_index("row")
    col_index = lax.axis_index("col")
    strip_rows = start_strip.shape[1]
    strip_cols = start_strip.shape[2]
    group_rows = strip_rows * col_count
    tile_cols = history.shape[2]
    share_cols = tile_cols // row_count
    sigma_first = self_energy(
        start_strip,
        orbital_weights(coupling, col_index * strip_rows, strip_rows),
        orbital_weights(coupling, row_index * strip_cols, strip_cols),
    ).astype(jnp.bfloat16)
    fits = share_cols % 128 == 0
    if fits:
        shares = first_sums(sigma_first, history, col_count // 2, row_count)
    else:
        partial_first = complex_product(
            lax.all_gather(sigma_first, "col", axis=1, tiled=True), history
        )
        shares = lax.psum_scatter(partial_first, "row", scatter_dimension=2, tiled=True)
    solved_part = stacked_dyson(dyson_inverse[0], shares)
    sigma_second = self_energy(
        solved_part,
        orbital_weights(coupling, 0, group_rows),
        orbital_weights(coupling, col_index * tile_cols + row_index * share_cols, share_cols),
    ).astype(jnp.bfloat16)
    solved_sigma = stacked_dyson(
        dyson_inverse[1], sigma_second.astype(jnp.float32)
    ).astype(jnp.bfloat16)
    if fits:
        later_strip, wide = second_sums(
            solved_sigma, solved_part.astype(jnp.bfloat16), history, col_count // 2, row_count
        )
        return (wide.astype(jnp.float32), later_strip)
    earlier = lax.all_gather(solved_part, "row", axis=2, tiled=True)
    tau = lax.all_gather(solved_sigma, "row", axis=2, tiled=True)
    partial_second = mirror_product(tau, history)
    later_strip = lax.psum_scatter(partial_second, "col", scatter_dimension=1, tiled=True)
    return (earlier, later_strip)


def solution(mesh):
    return jax.shard_map(
        shards,
        mesh=mesh,
        in_specs=(P(None, "row", "col"), P(None, "col", "row"), P(), P()),
        out_specs=(P(None, None, "col"), P(None, "col", "row")),
        check_vma=False,
    )
```
